256 devices in a mesh: row: 16 (over x, y_lo, core), col: 16 (over z, y_hi).
Axes of the slice: x: 4, y: 4 (y_hi: 2, y_lo: 2; y = y_hi * 2 + y_lo), z: 8, core: 2. Of those that a mesh axis runs over, the one named last changes fastest.
Arguments:
- ancestor_inverse: float32 [24576, 24576], P('row', 'col'), may hold values from -1 to 5, as said below
- factor_panel: float32 [24576, 512], P('row'), may hold values from -6 to 6
- ancestor_blocks: int32 [16, 12], replicated, may hold values from 0 to 11, each once within a row
- ancestor_count: int32 [16], replicated, may hold values from 1 to 12, 128 in all
Outputs:
- inverse_panel: float32 [24576, 512], P(('row', 'col'))
- inverse_row: float32 [512, 24576], P('row', 'col')
The draws below stay inside these ranges and needn't reach their ends.
Inputs may be any that keep to these rules, and one draw needn't show every extreme that they name: ancestor_inverse is symmetric: equal to its transpose. `ancestor_blocks`: each row is an ordering of the 12 blocks of one tile. `ancestor_count`: the counts sum to 128, and some tile has all 12 slots live.
All inputs are finite; a program needn't handle non-finite values.
Results may differ from the reference program's by a relative error of at most 0.000071.
Values sent between devices are 32-bit elements; how exact they have to be, the bound alone decides.
No kernel may reach another device: no remote copies, remote signals or barrier semaphores. Data moves between devices by JAX's collectives and lax.ppermute only.
A program may use at most 128 MiB of HBM per device.

```python
import math
import jax
import jax.numpy as jnp
import numpy as np
from jax import lax

SUPER = 512
BLOCK = 128
TILE_BLOCKS = 12
ORDER = 24576
N_ROW = 16


def draw_ancestor_inverse(key, part):
    random_part = jax.random.truncated_normal(key, -4.0, 4.0, (ORDER, ORDER), jnp.float32)
    symmetric = (random_part + random_part.T) * (0.5 / jnp.sqrt(jnp.float32(ORDER)))
    diagonal_ids = jnp.arange(ORDER)
    symmetric = symmetric.at[diagonal_ids, diagonal_ids].add(1.0)
    return symmetric


def steps_of(stream_key, extent, pieces, least, high):
    gain, own = 1.0, jax.random.fold_in(stream_key, 6)
    for position, shards_of in pieces:
        heights = jnp.exp(jax.random.uniform(jax.random.fold_in(own, position), (shards_of,), jnp.float32, least / len(pieces), high / len(pieces)))
        gain = gain * jnp.repeat(heights, extent[position] // shards_of).reshape([-1 if axis == position else 1 for axis in range(len(extent))])
    return gain


def length_profile(count, total, bound, skew):
    portions = [(1 << 20) // math.isqrt(rank ** skew) + 1 for rank in range(2, count + 1)]
    spare, holding = total - bound - (count - 1), [1] * (count - 1)
    while spare > 0:
        free = [i for i in range(count - 1) if holding[i] < bound]
        pool, budget = sum([portions[i] for i in free]), spare
        for i in free:
            extra = min(bound - holding[i], max(1, budget * portions[i] // pool), spare)
            holding[i] = holding[i] + extra
            spare = spare - extra
    return np.array([bound] + holding)


def ragged_sizes(own_key, amount, total, reach, lean):
    if amount == 2:
        one = jax.random.randint(own_key, (), max(1, total - reach), min(reach, total - 1) + 1)
        return jnp.stack([one, total - one])
    sizes = jnp.asarray(length_profile(amount, total, reach, lean), jnp.int32)
    twos = (amount - 1) // 2
    giver, receiver = sizes[1:1 + 2 * twos:2], sizes[2:2 + 2 * twos:2]
    margin = jnp.minimum(giver - 1, reach - receiver)
    shifted = jax.random.randint(jax.random.fold_in(own_key, 1), (twos,), 0, 1 << 20) % (margin + 1)
    sizes = sizes.at[1:1 + 2 * twos:2].set(giver - shifted).at[2:2 + 2 * twos:2].set(receiver + shifted)
    return sizes[jax.random.permutation(jax.random.fold_in(own_key, 2), amount)]


def scatter_about(rng, extent, width, most, pieces=(), dtype=jnp.bfloat16):
    entries = width * jax.random.normal(rng, extent, jnp.float32)
    if pieces:
        entries = entries * steps_of(rng, extent, pieces, -0.22, 0.18)
    return jnp.clip(entries, -most, most).astype(dtype)


def setup_inputs(seed: int = 0) -> dict:
    arg_keys = jax.random.split(jax.random.key(seed), 5)
    ancestor_inverse = draw_ancestor_inverse(jax.random.fold_in(arg_keys[4], 71), 0)
    factor_panel = scatter_about(arg_keys[1], (ORDER, SUPER), 1.0, 6.0, ((0, 16),), jnp.float32)
    ancestor_blocks = jax.vmap(lambda own: jax.random.permutation(own, TILE_BLOCKS))(jax.random.split(arg_keys[2], N_ROW)).reshape((N_ROW, TILE_BLOCKS)).astype(jnp.int32)
    ancestor_count = ragged_sizes(arg_keys[3], N_ROW, N_ROW * TILE_BLOCKS * 2 // 3, TILE_BLOCKS, 2).astype(jnp.int32)
    return {"ancestor_inverse": ancestor_inverse, "factor_panel": factor_panel, "ancestor_blocks": ancestor_blocks, "ancestor_count": ancestor_count}


def reference(ancestor_inverse, factor_panel, ancestor_blocks, ancestor_count):
    tile_rows = TILE_BLOCKS * BLOCK
    slot_ids = lax.iota(jnp.int32, TILE_BLOCKS)
    active = slot_ids[None, :] < ancestor_count[:, None]
    tile_start = (lax.iota(jnp.int32, N_ROW) * tile_rows)[:, None, None]
    within = lax.iota(jnp.int32, BLOCK)[None, None, :]
    natural = (tile_start + ancestor_blocks[:, :, None] * BLOCK + within).reshape(-1).astype(jnp.int32)
    keep = jnp.broadcast_to(active[:, :, None], (N_ROW, TILE_BLOCKS, BLOCK)).reshape(-1).astype(jnp.float32)
    masked = factor_panel * keep[:, None]
    spread = jnp.zeros_like(factor_panel).at[natural].set(masked)
    applied = jnp.dot(ancestor_inverse, spread, precision=lax.Precision.HIGHEST, preferred_element_type=jnp.float32)
    inverse_panel = -applied[natural] * keep[:, None]
    return inverse_panel, inverse_panel.T
```

```python
import jax
import jax.numpy as jnp
from jax import lax
from jax.experimental import pallas as pl
from jax.experimental.pallas import tpu as pltpu
from jax.sharding import PartitionSpec as P


def product_kernel(table, a_hbm, f_ref, keep_ref, send_ref, a_buf, f_high, f_low, acc, sems):
    slots = sems.shape[0]
    tile_rows, width = f_ref.shape
    block = tile_rows // slots
    share = keep_ref.shape[1]
    group_rows = acc.shape[0]
    group_slots = group_rows // block
    pairs = group_rows // (2 * share)
    own_count, col_count, core = table[2, 0], table[2, 1], table[2, 2]

    def column_copy(s):
        start = pl.multiple_of(table[1, s] * block, block)
        return pltpu.make_async_copy(
            a_hbm.at[:, pl.ds(start, block)],
            a_buf.at[s // group_slots, :, pl.ds(pl.multiple_of((s % group_slots) * block, block), block)],
            sems.at[s],
        )

    @pl.loop(0, slots)
    def _(s):
        column_copy(s).start()

    @pl.loop(0, slots)
    def _(s):
        rows = f_ref[pl.ds(pl.multiple_of(s * block, block), block), :]
        rows = jnp.where(s < own_count, -rows, 0.0)
        high = rows.astype(jnp.bfloat16)
        target = pl.ds(pl.multiple_of(table[0, s] * block, block), block)
        f_high[target, :] = high
        f_low[target, :] = (rows - high.astype(jnp.float32)).astype(jnp.bfloat16)

    dims = (((0,), (0,)), ((), ()))

    def product(a, f):
        return lax.dot_general(a, f, dims, preferred_element_type=jnp.float32)

    @pl.loop(0, slots // group_slots)
    def _(g):
        for i in range(group_slots):
            column_copy(g * group_slots + i).wait()
        a = a_buf[g]
        high = a.astype(jnp.bfloat16)
        low = (a - high.astype(jnp.float32)).astype(jnp.bfloat16)
        total = product(low, f_high[...]) + product(high, f_low[...]) + product(high, f_high[...])
        row_slot = g * group_slots + lax.broadcasted_iota(jnp.int32, (group_rows, 1), 0) // block
        acc[...] = jnp.where(row_slot < col_count, total, 0.0)
        for j in range(pairs):
            keep_ref[g * pairs + j] = acc[pl.ds((2 * j + core) * share, share), :]
            send_ref[g * pairs + j] = acc[pl.ds((2 * j + 1 - core) * share, share), :]


def partial_product(table, a, f, shares):
    tile_rows, width = f.shape
    slots = table.shape[1]
    share = tile_rows // shares
    half = jax.ShapeDtypeStruct((shares // 2, share, width), jnp.float32)
    group_rows = tile_rows // 4
    return pl.pallas_call(
        product_kernel,
        out_shape=(half, half),
        in_specs=[
            pl.BlockSpec(memory_space=pltpu.SMEM),
            pl.BlockSpec(memory_space=pl.ANY),
            pl.BlockSpec(memory_space=pltpu.VMEM),
        ],
        out_specs=(pl.BlockSpec(memory_space=pltpu.VMEM), pl.BlockSpec(memory_space=pltpu.VMEM)),
        scratch_shapes=[
            pltpu.VMEM((4, tile_rows, group_rows), jnp.float32),
            pltpu.VMEM((tile_rows, width), jnp.bfloat16),
            pltpu.VMEM((tile_rows, width), jnp.bfloat16),
            pltpu.VMEM((group_rows, width), jnp.float32),
            pltpu.SemaphoreType.DMA((slots,)),
        ],
        compiler_params=pltpu.CompilerParams(vmem_limit_bytes=48 * 1024 * 1024),
        name="partial_product",
    )(table, a, f)


def per_device(ancestor_inverse, factor_panel, ancestor_blocks, ancestor_count):
    rows, cols = lax.axis_size("row"), lax.axis_size("col")
    r, c = lax.axis_index("row"), lax.axis_index("col")
    width = factor_panel.shape[1]
    slots = ancestor_blocks.shape[1]
    core = r % 2
    pick = lambda array, i: lax.dynamic_index_in_dim(array, i, 0, keepdims=False)
    scalars = jnp.stack([pick(ancestor_count, r), pick(ancestor_count, c), core.astype(jnp.int32)])
    table = jnp.stack([pick(ancestor_blocks, r), pick(ancestor_blocks, c), jnp.pad(scalars, (0, slots - 3))])
    keep, send = partial_product(table, ancestor_inverse, factor_panel, rows)
    arrived = lax.ppermute(send, "row", [(i, i ^ 1) for i in range(rows)])
    chip_sum = keep + arrived
    groups = [[i for i in range(rows) if i % 2 == k] for k in range(2)]
    parts = lax.all_to_all(chip_sum, "row", 0, 0, axis_index_groups=groups, tiled=True)
    share = parts.sum(axis=0)
    swap = [(i * cols + j, j * cols + i) for i in range(rows) for j in range(cols)]
    inverse_panel = lax.ppermute(share, ("row", "col"), swap)
    features = share.T.reshape(rows, width // rows, share.shape[0])
    mirrored = lax.all_to_all(features, "row", 0, 2, tiled=True)
    return inverse_panel, mirrored.reshape(width // rows, rows * share.shape[0])


def solution(mesh):
    return jax.shard_map(
        per_device,
        mesh=mesh,
        in_specs=(P("row", "col"), P("row", None), P(), P()),
        out_specs=(P(("row", "col"), None), P("row", "col")),
        check_vma=False,
    )
```

```python
import functools

import jax
import jax.numpy as jnp
from jax import lax
from jax.experimental import pallas as pl
from jax.experimental.pallas import tpu as pltpu
from jax.sharding import PartitionSpec as P


RING = 4
PIECES = 2
ORDER = (2, 1, 3, 0)


def emit_chunk(blocks_count, chunk, a, f_high, f_low, acc, keep_ref, send_ref):
    block, count = blocks_count
    share = keep_ref.shape[1]
    rows = acc.shape[0]
    dims = (((0,), (0,)), ((), ()))

    def product(left, right):
        return lax.dot_general(left, right, dims, preferred_element_type=jnp.float32)

    high = a.astype(jnp.bfloat16)
    low = (a - high.astype(jnp.float32)).astype(jnp.bfloat16)
    total = product(low, f_high[...]) + product(high, f_low[...]) + product(high, f_high[...])
    slot = chunk * (rows // block) + lax.broadcasted_iota(jnp.int32, (rows, 1), 0) // block
    acc[...] = jnp.where(slot < count, total, 0.0)
    r = lax.axis_index("row")
    core, y = r % 2, (r // 2) % 2
    for other in range(2):
        pair = 2 * jnp.where(other == 0, y, 1 - y)
        keep_ref[other] = acc[pl.ds((pair + core) * share, share), :]
        send_ref[other] = acc[pl.ds((pair + 1 - core) * share, share), :]


def column_copies(ahead, blocks, a_hbm, target, sems):
    tile_rows, chunk_rows = target.shape
    slots = blocks.shape[1]
    block = tile_rows // slots
    per_chunk = chunk_rows // block
    chunk = (lax.axis_index("row") // 4 + ahead) % RING
    copies = []
    for i in range(per_chunk):
        start = pl.multiple_of(blocks[lax.axis_index("col"), chunk * per_chunk + i] * block, block)
        copies.append(
            pltpu.make_async_copy(
                a_hbm.at[:, pl.ds(start, block)], target.at[:, pl.ds(i * block, block)], sems.at[i]
            )
        )
    return copies


def first_kernel(blocks_hbm, counts_hbm, a_hbm, f_hbm, keep_ref, send_ref, a_1, a_2, a_3, f_high, f_low, *scratch):
    a_buf, f_buf, acc, blocks, counts, a_sems, f_sems, table_sems = scratch
    slots = f_sems.shape[0]
    tile_rows = f_buf.shape[0]
    block = tile_rows // slots
    r, c = lax.axis_index("row"), lax.axis_index("col")
    tables = [
        pltpu.make_async_copy(blocks_hbm, blocks, table_sems.at[0]),
        pltpu.make_async_copy(counts_hbm, counts, table_sems.at[1]),
    ]
    for copy in tables:
        copy.start()

    def f_copy(s):
        span = pl.ds(pl.multiple_of(s * block, block), block)
        return pltpu.make_async_copy(f_hbm.at[span, :], f_buf.at[span, :], f_sems.at[s])

    for s in range(slots):
        f_copy(s).start()
    for copy in tables:
        copy.wait()
    now, *later = [
        column_copies(ahead, blocks, a_hbm, target, a_sems.at[i])
        for i, (ahead, target) in enumerate(zip(ORDER, (a_buf, a_1, a_2, a_3)))
    ]
    for copies in (now, *later):
        for copy in copies:
            copy.start()
    own_count = counts[r]

    @pl.loop(0, slots)
    def _(s):
        f_copy(s).wait()
        rows = f_buf[pl.ds(pl.multiple_of(s * block, block), block), :]
        rows = jnp.where(s < own_count, -rows, 0.0)
        high = rows.astype(jnp.bfloat16)
        target = pl.ds(pl.multiple_of(blocks[r, s] * block, block), block)
        f_high[target, :] = high
        f_low[target, :] = (rows - high.astype(jnp.float32)).astype(jnp.bfloat16)

    for copy in now:
        copy.wait()
    chunk = (r // 4 + ORDER[0]) % RING
    emit_chunk((block, counts[c]), chunk, a_buf[...], f_high, f_low, acc, keep_ref, send_ref)
    for copies in later:
        for copy in copies:
            copy.wait()


def next_kernel(step, slots, counts, a_now, f_high, f_low, keep_ref, send_ref, acc):
    block = a_now.shape[0] // slots
    chunk = (lax.axis_index("row") // 4 + ORDER[step]) % RING
    emit_chunk((block, counts[lax.axis_index("col")]), chunk, a_now[...], f_high, f_low, acc, keep_ref, send_ref)


SMEM = pl.BlockSpec(memory_space=pltpu.SMEM)
VMEM = pl.BlockSpec(memory_space=pltpu.VMEM)
HBM = pl.BlockSpec(memory_space=pltpu.HBM)
PARAMS = pltpu.CompilerParams(vmem_limit_bytes=24 * 1024 * 1024)


def chunk_products(blocks, counts, a, f, share):
    tile_rows, width = f.shape
    slots = blocks.shape[1]
    chunk_rows = tile_rows // RING
    per_chunk = slots // RING
    half = jax.ShapeDtypeStruct((2, share, width), jnp.float32)
    split = jax.ShapeDtypeStruct((tile_rows, width), jnp.bfloat16)
    columns = jax.ShapeDtypeStruct((tile_rows, chunk_rows), jnp.float32)
    acc = pltpu.VMEM((chunk_rows, width), jnp.float32)
    in_hbm = [pltpu.with_memory_space_constraint(value, pltpu.HBM) for value in (blocks, counts, a, f)]
    keep, send, *columns_of, high, low = pl.pallas_call(
        first_kernel,
        out_shape=(half, half, columns, columns, columns, split, split),
        in_specs=[HBM] * 4,
        out_specs=(VMEM,) * 7,
        scratch_shapes=[
            pltpu.VMEM((tile_rows, chunk_rows), jnp.float32),
            pltpu.VMEM((tile_rows, width), jnp.float32),
            acc,
            pltpu.SMEM(blocks.shape, jnp.int32),
            pltpu.SMEM(counts.shape, jnp.int32),
            pltpu.SemaphoreType.DMA((RING, per_chunk)),
            pltpu.SemaphoreType.DMA((slots,)),
            pltpu.SemaphoreType.DMA((2,)),
        ],
        compiler_params=PARAMS,
        name="product_0",
    )(*in_hbm)
    yield keep, send
    for step in range(1, RING):
        yield pl.pallas_call(
            functools.partial(next_kernel, step, slots),
            out_shape=(half, half),
            in_specs=[SMEM, VMEM, VMEM, VMEM],
            out_specs=(VMEM, VMEM),
            scratch_shapes=[acc],
            compiler_params=PARAMS,
        )(counts, columns_of[step - 1], high, low)


def per_device(ancestor_inverse, factor_panel, ancestor_blocks, ancestor_count):
    rows, cols = lax.axis_size("row"), lax.axis_size("col")
    width = factor_panel.shape[1]
    share_rows = factor_panel.shape[0] // rows
    piece = width // PIECES
    along_x = rows // RING

    def to(value, target):
        return lax.ppermute(value, "row", [(i, target(i)) for i in range(rows)])

    def ahead(value):
        return to(value, lambda i: (i + along_x) % rows)

    def behind(value):
        return to(value, lambda i: (i - along_x) % rows)

    products = list(chunk_products(ancestor_blocks, ancestor_count, ancestor_inverse, factor_panel, share_rows))
    far, front, back, own = [keep + to(send, lambda i: i ^ 1) for keep, send in products]
    from_back, from_front = ahead(far[0]), behind(far[1])
    swap = [(i * cols + j, j * cols + i) for i in range(rows) for j in range(cols)]
    arrivals = []
    for p in range(PIECES):
        part = slice(p * piece, (p + 1) * piece)
        plus = jnp.stack([front[0, :, part] + from_back[:, part], front[1, :, part]])
        minus = jnp.stack([back[0, :, part], back[1, :, part] + from_front[:, part]])
        front, back, plus, minus = lax.optimization_barrier((front, back, plus, minus))
        arrivals.append((own[:, :, part], ahead(plus), behind(minus)))
    halves = []
    for p in range(PIECES):
        total = sum(arrivals[p])
        if p + 1 < PIECES:
            total, arrivals[p + 1] = lax.optimization_barrier((total, (arrivals[p + 1][0],))), arrivals[p + 1]
            total, (following,) = total
            arrivals[p + 1] = (following,) + arrivals[p + 1][1:]
        halves.append((total[0], to(total[1], lambda i: i ^ 2)))
    shares, panels = [], []
    for p in range(PIECES):
        mine, other = halves[p]
        share = mine + other
        if p + 1 < PIECES:
            share, following = lax.optimization_barrier((share, halves[p + 1][0]))
            halves[p + 1] = (following, halves[p + 1][1])
        shares.append(share)
        panels.append(lax.ppermute(share, ("row", "col"), swap))
    share = jnp.concatenate(shares, axis=1)
    features = share.T.reshape(rows, width // rows, share_rows)
    mirrored = lax.all_to_all(features, "row", 0, 2, tiled=True)
    return jnp.concatenate(panels, axis=1), mirrored.reshape(width // rows, rows * share_rows)


def solution(mesh):
    return jax.shard_map(
        per_device,
        mesh=mesh,
        in_specs=(P("row", "col"), P("row", None), P(), P()),
        out_specs=(P(("row", "col"), None), P("row", "col")),
        check_vma=False,
    )
```

```python
import functools

import jax
import jax.numpy as jnp
from jax import lax
from jax.experimental import pallas as pl
from jax.experimental.pallas import tpu as pltpu
from jax.sharding import PartitionSpec as P


RING = 4
PIECES = 2
ORDER = (2, 1, 3, 0)


def chunk_of(x, c):
    return (2 * (c // RING) + 2 * RING + 2 - x) % RING


def share_of(r, c):
    return RING * chunk_of(r // RING, c) + 2 * (r % 2) + (r // 2) % 2


def emit_chunk(blocks_count, chunk, a, f_high, f_low, acc, keep_ref, send_ref):
    block, count = blocks_count
    share = keep_ref.shape[1]
    rows = acc.shape[0]
    dims = (((0,), (0,)), ((), ()))

    def product(left, right):
        return lax.dot_general(left, right, dims, preferred_element_type=jnp.float32)

    high = a.astype(jnp.bfloat16)
    low = (a - high.astype(jnp.float32)).astype(jnp.bfloat16)
    total = product(low, f_high[...]) + product(high, f_low[...]) + product(high, f_high[...])
    slot = chunk * (rows // block) + lax.broadcasted_iota(jnp.int32, (rows, 1), 0) // block
    acc[...] = jnp.where(slot < count, total, 0.0)
    r = lax.axis_index("row")
    core, y = r % 2, (r // 2) % 2
    for other in range(2):
        along_y = y if other == 0 else 1 - y
        keep_ref[other] = acc[pl.ds((2 * core + along_y) * share, share), :]
        send_ref[other] = acc[pl.ds((2 * (1 - core) + along_y) * share, share), :]


def column_copies(ahead, blocks, a_hbm, target, sems):
    tile_rows, chunk_rows = target.shape
    slots = blocks.shape[1]
    block = tile_rows // slots
    per_chunk = chunk_rows // block
    chunk = chunk_of(lax.axis_index("row") // 4 + ahead, lax.axis_index("col"))
    copies = []
    for i in range(per_chunk):
        start = pl.multiple_of(blocks[lax.axis_index("col"), chunk * per_chunk + i] * block, block)
        copies.append(
            pltpu.make_async_copy(
                a_hbm.at[:, pl.ds(start, block)], target.at[:, pl.ds(i * block, block)], sems.at[i]
            )
        )
    return copies


def first_kernel(blocks_hbm, counts_hbm, a_hbm, f_hbm, keep_ref, send_ref, a_1, a_2, a_3, f_high, f_low, *scratch):
    a_buf, f_buf, acc, blocks, counts, a_sems, f_sems, table_sems = scratch
    slots = f_sems.shape[0]
    tile_rows = f_buf.shape[0]
    block = tile_rows // slots
    r, c = lax.axis_index("row"), lax.axis_index("col")
    tables = [
        pltpu.make_async_copy(blocks_hbm, blocks, table_sems.at[0]),
        pltpu.make_async_copy(counts_hbm, counts, table_sems.at[1]),
    ]
    for copy in tables:
        copy.start()

    def f_copy(s):
        span = pl.ds(pl.multiple_of(s * block, block), block)
        return pltpu.make_async_copy(f_hbm.at[span, :], f_buf.at[span, :], f_sems.at[s])

    for s in range(slots):
        f_copy(s).start()
    for copy in tables:
        copy.wait()
    now, *later = [
        column_copies(ahead, blocks, a_hbm, target, a_sems.at[i])
        for i, (ahead, target) in enumerate(zip(ORDER, (a_buf, a_1, a_2, a_3)))
    ]
    for copies in (now, *later):
        for copy in copies:
            copy.start()
    own_count = counts[r]

    @pl.loop(0, slots)
    def _(s):
        f_copy(s).wait()
        rows = f_buf[pl.ds(pl.multiple_of(s * block, block), block), :]
        rows = jnp.where(s < own_count, -rows, 0.0)
        high = rows.astype(jnp.bfloat16)
        target = pl.ds(pl.multiple_of(blocks[r, s] * block, block), block)
        f_high[target, :] = high
        f_low[target, :] = (rows - high.astype(jnp.float32)).astype(jnp.bfloat16)

    for copy in now:
        copy.wait()
    chunk = chunk_of(r // 4 + ORDER[0], c)
    emit_chunk((block, counts[c]), chunk, a_buf[...], f_high, f_low, acc, keep_ref, send_ref)
    for copies in later:
        for copy in copies:
            copy.wait()


def next_kernel(step, slots, counts, a_now, f_high, f_low, keep_ref, send_ref, acc):
    block = a_now.shape[0] // slots
    c = lax.axis_index("col")
    chunk = chunk_of(lax.axis_index("row") // 4 + ORDER[step], c)
    emit_chunk((block, counts[c]), chunk, a_now[...], f_high, f_low, acc, keep_ref, send_ref)


SMEM = pl.BlockSpec(memory_space=pltpu.SMEM)
VMEM = pl.BlockSpec(memory_space=pltpu.VMEM)
HBM = pl.BlockSpec(memory_space=pltpu.HBM)
PARAMS = pltpu.CompilerParams(vmem_limit_bytes=24 * 1024 * 1024)


def chunk_products(blocks, counts, a, f, share):
    tile_rows, width = f.shape
    slots = blocks.shape[1]
    chunk_rows = tile_rows // RING
    per_chunk = slots // RING
    half = jax.ShapeDtypeStruct((2, share, width), jnp.float32)
    split = jax.ShapeDtypeStruct((tile_rows, width), jnp.bfloat16)
    columns = jax.ShapeDtypeStruct((tile_rows, chunk_rows), jnp.float32)
    acc = pltpu.VMEM((chunk_rows, width), jnp.float32)
    in_hbm = [pltpu.with_memory_space_constraint(value, pltpu.HBM) for value in (blocks, counts, a, f)]
    keep, send, *columns_of, high, low = pl.pallas_call(
        first_kernel,
        out_shape=(half, half, columns, columns, columns, split, split),
        in_specs=[HBM] * 4,
        out_specs=(VMEM,) * 7,
        scratch_shapes=[
            pltpu.VMEM((tile_rows, chunk_rows), jnp.float32),
            pltpu.VMEM((tile_rows, width), jnp.float32),
            acc,
            pltpu.SMEM(blocks.shape, jnp.int32),
            pltpu.SMEM(counts.shape, jnp.int32),
            pltpu.SemaphoreType.DMA((RING, per_chunk)),
            pltpu.SemaphoreType.DMA((slots,)),
            pltpu.SemaphoreType.DMA((2,)),
        ],
        compiler_params=PARAMS,
        name="product_0",
    )(*in_hbm)
    yield keep, send
    for step in range(1, RING):
        yield pl.pallas_call(
            functools.partial(next_kernel, step, slots),
            out_shape=(half, half),
            in_specs=[SMEM, VMEM, VMEM, VMEM],
            out_specs=(VMEM, VMEM),
            scratch_shapes=[acc],
            compiler_params=PARAMS,
        )(counts, columns_of[step - 1], high, low)


def per_device(ancestor_inverse, factor_panel, ancestor_blocks, ancestor_count):
    rows, cols = lax.axis_size("row"), lax.axis_size("col")
    width = factor_panel.shape[1]
    share_rows = factor_panel.shape[0] // rows
    piece = width // PIECES
    along_x = rows // RING

    def to(value, target):
        return lax.ppermute(value, "row", [(i, target(i)) for i in range(rows)])

    def ahead(value):
        return to(value, lambda i: (i + along_x) % rows)

    def behind(value):
        return to(value, lambda i: (i - along_x) % rows)

    products = list(chunk_products(ancestor_blocks, ancestor_count, ancestor_inverse, factor_panel, share_rows))
    far, front, back, own = [keep + to(send, lambda i: i ^ 1) for keep, send in products]
    from_back, from_front = ahead(far[0]), behind(far[1])
    swap = [(i * cols + j, j * cols + share_of(i, j)) for i in range(rows) for j in range(cols)]
    arrivals = []
    for p in range(PIECES):
        part = slice(p * piece, (p + 1) * piece)
        plus = jnp.stack([front[0, :, part] + from_back[:, part], front[1, :, part]])
        minus = jnp.stack([back[0, :, part], back[1, :, part] + from_front[:, part]])
        front, back, plus, minus = lax.optimization_barrier((front, back, plus, minus))
        arrivals.append((own[:, :, part], ahead(plus), behind(minus)))
    halves = []
    for p in range(PIECES):
        total = sum(arrivals[p])
        if p + 1 < PIECES:
            total, arrivals[p + 1] = lax.optimization_barrier((total, (arrivals[p + 1][0],))), arrivals[p + 1]
            total, (following,) = total
            arrivals[p + 1] = (following,) + arrivals[p + 1][1:]
        halves.append((total[0], to(total[1], lambda i: i ^ 2)))
    shares = []
    for p in range(PIECES):
        mine, other = halves[p]
        share = mine + other
        if p + 1 < PIECES:
            share, following = lax.optimization_barrier((share, halves[p + 1][0]))
            halves[p + 1] = (following, halves[p + 1][1])
        shares.append(share)
    share = jnp.concatenate(shares, axis=1)
    inverse_panel = lax.ppermute(share, ("row", "col"), swap)
    features = share.T.reshape(rows, width // rows, share_rows)
    pieces = lax.all_to_all(features, "row", 0, 0, tiled=True)
    return inverse_panel, in_order(pieces)


def in_order_kernel(pieces, out):
    rows = pieces.shape[0]
    c = lax.axis_index("col")
    parts = []
    for s in range(rows):
        x = (2 * (c // RING) + 2 * RING + 2 - s // RING) % RING
        parts.append(pieces[RING * x + 2 * (s % 2) + (s // 2) % 2])
    out[...] = jnp.concatenate(parts, axis=1)


def in_order(pieces):
    count, height, columns = pieces.shape
    return pl.pallas_call(
        in_order_kernel,
        out_shape=jax.ShapeDtypeStruct((height, count * columns), pieces.dtype),
        in_specs=[VMEM],
        out_specs=VMEM,
        compiler_params=pltpu.CompilerParams(vmem_limit_bytes=8 * 1024 * 1024),
        name="in_order",
    )(pieces)


def solution(mesh):
    return jax.shard_map(
        per_device,
        mesh=mesh,
        in_specs=(P("row", "col"), P("row", None), P(), P()),
        out_specs=(P(("row", "col"), None), P("row", "col")),
        check_vma=False,
    )
```

```python
import functools

import jax
import jax.numpy as jnp
from jax import lax
from jax.experimental import pallas as pl
from jax.experimental.pallas import tpu as pltpu
from jax.sharding import PartitionSpec as P


RING = 4
ORDER = (2, 1, 3, 0)


def chunk_of(x, c):
    return (2 * (c // RING) + 2 * RING + 2 - x) % RING


def share_of(r, c):
    return RING * chunk_of(r // RING, c) + 2 * (r % 2) + (r // 2) % 2


def emit_chunk(blocks_count, chunk, a, f_high, f_low, acc, keep_ref, send_ref):
    block, count = blocks_count
    share = keep_ref.shape[1]
    rows = acc.shape[0]
    dims = (((0,), (0,)), ((), ()))

    def product(left, right):
        return lax.dot_general(left, right, dims, preferred_element_type=jnp.float32)

    high = a.astype(jnp.bfloat16)
    low = (a - high.astype(jnp.float32)).astype(jnp.bfloat16)
    total = product(low, f_high[...]) + product(high, f_low[...]) + product(high, f_high[...])
    slot = chunk * (rows // block) + lax.broadcasted_iota(jnp.int32, (rows, 1), 0) // block
    acc[...] = jnp.where(slot < count, total, 0.0)
    r = lax.axis_index("row")
    core, y = r % 2, (r // 2) % 2
    for other in range(2):
        along_y = y if other == 0 else 1 - y
        keep_ref[other] = acc[pl.ds((2 * core + along_y) * share, share), :]
        send_ref[other] = acc[pl.ds((2 * (1 - core) + along_y) * share, share), :]


def column_copies(ahead, blocks, a_hbm, target, sems):
    tile_rows, chunk_rows = target.shape
    slots = blocks.shape[1]
    block = tile_rows // slots
    per_chunk = chunk_rows // block
    chunk = chunk_of(lax.axis_index("row") // 4 + ahead, lax.axis_index("col"))
    copies = []
    for i in range(per_chunk):
        start = pl.multiple_of(blocks[lax.axis_index("col"), chunk * per_chunk + i] * block, block)
        copies.append(
            pltpu.make_async_copy(
                a_hbm.at[:, pl.ds(start, block)], target.at[:, pl.ds(i * block, block)], sems.at[i]
            )
        )
    return copies


def first_kernel(blocks_hbm, counts_hbm, a_hbm, f_hbm, keep_ref, send_ref, a_1, a_2, a_3, f_high, f_low, *scratch):
    a_buf, f_buf, acc, blocks, counts, a_sems, f_sems, table_sems = scratch
    slots = f_sems.shape[0]
    tile_rows = f_buf.shape[0]
    block = tile_rows // slots
    r, c = lax.axis_index("row"), lax.axis_index("col")
    tables = [
        pltpu.make_async_copy(blocks_hbm, blocks, table_sems.at[0]),
        pltpu.make_async_copy(counts_hbm, counts, table_sems.at[1]),
    ]
    for copy in tables:
        copy.start()

    def f_copy(s):
        span = pl.ds(pl.multiple_of(s * block, block), block)
        return pltpu.make_async_copy(f_hbm.at[span, :], f_buf.at[span, :], f_sems.at[s])

    for s in range(slots):
        f_copy(s).start()
    for copy in tables:
        copy.wait()
    now, *later = [
        column_copies(ahead, blocks, a_hbm, target, a_sems.at[i])
        for i, (ahead, target) in enumerate(zip(ORDER, (a_buf, a_1, a_2, a_3)))
    ]
    for copies in (now, *later):
        for copy in copies:
            copy.start()
    own_count = counts[r]

    @pl.loop(0, slots)
    def _(s):
        f_copy(s).wait()
        rows = f_buf[pl.ds(pl.multiple_of(s * block, block), block), :]
        rows = jnp.where(s < own_count, -rows, 0.0)
        high = rows.astype(jnp.bfloat16)
        target = pl.ds(pl.multiple_of(blocks[r, s] * block, block), block)
        f_high[target, :] = high
        f_low[target, :] = (rows - high.astype(jnp.float32)).astype(jnp.bfloat16)

    for copy in now:
        copy.wait()
    chunk = chunk_of(r // 4 + ORDER[0], c)
    emit_chunk((block, counts[c]), chunk, a_buf[...], f_high, f_low, acc, keep_ref, send_ref)
    for copies in later:
        for copy in copies:
            copy.wait()


def next_kernel(step, slots, counts, a_now, f_high, f_low, keep_ref, send_ref, acc):
    block = a_now.shape[0] // slots
    c = lax.axis_index("col")
    chunk = chunk_of(lax.axis_index("row") // 4 + ORDER[step], c)
    emit_chunk((block, counts[c]), chunk, a_now[...], f_high, f_low, acc, keep_ref, send_ref)


SMEM = pl.BlockSpec(memory_space=pltpu.SMEM)
VMEM = pl.BlockSpec(memory_space=pltpu.VMEM)
HBM = pl.BlockSpec(memory_space=pltpu.HBM)
PARAMS = pltpu.CompilerParams(vmem_limit_bytes=24 * 1024 * 1024)


def chunk_products(blocks, counts, a, f, share):
    tile_rows, width = f.shape
    slots = blocks.shape[1]
    chunk_rows = tile_rows // RING
    per_chunk = slots // RING
    half = jax.ShapeDtypeStruct((2, share, width), jnp.float32)
    split = jax.ShapeDtypeStruct((tile_rows, width), jnp.bfloat16)
    columns = jax.ShapeDtypeStruct((tile_rows, chunk_rows), jnp.float32)
    acc = pltpu.VMEM((chunk_rows, width), jnp.float32)
    in_hbm = [pltpu.with_memory_space_constraint(value, pltpu.HBM) for value in (blocks, counts, a, f)]
    keep, send, *columns_of, high, low = pl.pallas_call(
        first_kernel,
        out_shape=(half, half, columns, columns, columns, split, split),
        in_specs=[HBM] * 4,
        out_specs=(VMEM,) * 7,
        scratch_shapes=[
            pltpu.VMEM((tile_rows, chunk_rows), jnp.float32),
            pltpu.VMEM((tile_rows, width), jnp.float32),
            acc,
            pltpu.SMEM(blocks.shape, jnp.int32),
            pltpu.SMEM(counts.shape, jnp.int32),
            pltpu.SemaphoreType.DMA((RING, per_chunk)),
            pltpu.SemaphoreType.DMA((slots,)),
            pltpu.SemaphoreType.DMA((2,)),
        ],
        compiler_params=PARAMS,
        name="product_0",
    )(*in_hbm)
    yield keep, send
    for step in range(1, RING):
        yield pl.pallas_call(
            functools.partial(next_kernel, step, slots),
            out_shape=(half, half),
            in_specs=[SMEM, VMEM, VMEM, VMEM],
            out_specs=(VMEM, VMEM),
            scratch_shapes=[acc],
            compiler_params=PARAMS,
        )(counts, columns_of[step - 1], high, low)


def per_device(ancestor_inverse, factor_panel, ancestor_blocks, ancestor_count):
    rows, cols = lax.axis_size("row"), lax.axis_size("col")
    width = factor_panel.shape[1]
    share_rows = factor_panel.shape[0] // rows
    along_x = rows // RING

    def to(value, target):
        return lax.ppermute(value, "row", [(i, target(i)) for i in range(rows)])

    def ahead(value):
        return to(value, lambda i: (i + along_x) % rows)

    def behind(value):
        return to(value, lambda i: (i - along_x) % rows)

    products = list(chunk_products(ancestor_blocks, ancestor_count, ancestor_inverse, factor_panel, share_rows))

    def plane_sum(keep, send):
        chip = keep + to(send, lambda i: i ^ 1)
        return chip[0] + to(chip[1], lambda i: i ^ 2)

    far, front, back, own = [plane_sum(*product) for product in products]
    half = width // 2
    from_back, from_front = ahead(far[:, :half]), behind(far[:, half:])
    plus = jnp.concatenate([front[:, :half] + from_back, front[:, half:]], axis=1)
    minus = jnp.concatenate([back[:, :half], back[:, half:] + from_front], axis=1)
    share = own + ahead(plus) + behind(minus)
    swap = [(i * cols + j, j * cols + share_of(i, j)) for i in range(rows) for j in range(cols)]
    inverse_panel = lax.ppermute(share, ("row", "col"), swap)
    features = share.T.reshape(rows, width // rows, share_rows)
    pieces = lax.all_to_all(features, "row", 0, 0, tiled=True)
    return inverse_panel, in_order(pieces)


def in_order_kernel(pieces, out):
    rows = pieces.shape[0]
    c = lax.axis_index("col")
    parts = []
    for s in range(rows):
        x = (2 * (c // RING) + 2 * RING + 2 - s // RING) % RING
        parts.append(pieces[RING * x + 2 * (s % 2) + (s // 2) % 2])
    out[...] = jnp.concatenate(parts, axis=1)


def in_order(pieces):
    count, height, columns = pieces.shape
    return pl.pallas_call(
        in_order_kernel,
        out_shape=jax.ShapeDtypeStruct((height, count * columns), pieces.dtype),
        in_specs=[VMEM],
        out_specs=VMEM,
        compiler_params=pltpu.CompilerParams(vmem_limit_bytes=8 * 1024 * 1024),
        name="in_order",
    )(pieces)


def solution(mesh):
    return jax.shard_map(
        per_device,
        mesh=mesh,
        in_specs=(P("row", "col"), P("row", None), P(), P()),
        out_specs=(P(("row", "col"), None), P("row", "col")),
        check_vma=False,
    )
```

```python
import functools

import jax
import jax.numpy as jnp
from jax import lax
from jax.experimental import pallas as pl
from jax.experimental.pallas import tpu as pltpu
from jax.sharding import PartitionSpec as P


RING = 4
ORDER = (2, 1, 3, 0)


def chunk_of(x, c):
    return (2 * (c // RING) + 2 * RING + 2 - x) % RING


def share_of(r, c):
    return RING * chunk_of(r // RING, c) + 2 * (r % 2) + (r // 2) % 2


def emit_chunk(blocks_count, chunk, a, f_high, f_low, acc, keep_ref, send_ref):
    block, count = blocks_count
    share = keep_ref.shape[1]
    rows = acc.shape[0]
    dims = (((0,), (0,)), ((), ()))

    def product(left, right):
        return lax.dot_general(left, right, dims, preferred_element_type=jnp.float32)

    high = a.astype(jnp.bfloat16)
    low = (a - high.astype(jnp.float32)).astype(jnp.bfloat16)
    total = product(low, f_high[...]) + product(high, f_low[...]) + product(high, f_high[...])
    slot = chunk * (rows // block) + lax.broadcasted_iota(jnp.int32, (rows, 1), 0) // block
    acc[...] = jnp.where(slot < count, total, 0.0)
    r = lax.axis_index("row")
    core, y = r % 2, (r // 2) % 2
    for other in range(2):
        along_y = y if other == 0 else 1 - y
        keep_ref[other] = acc[pl.ds((2 * core + along_y) * share, share), :]
        send_ref[other] = acc[pl.ds((2 * (1 - core) + along_y) * share, share), :]


def column_copies(ahead, blocks, a_hbm, target, sems):
    tile_rows, chunk_rows = target.shape
    slots = blocks.shape[1]
    block = tile_rows // slots
    per_chunk = chunk_rows // block
    chunk = chunk_of(lax.axis_index("row") // 4 + ahead, lax.axis_index("col"))
    copies = []
    for i in range(per_chunk):
        start = pl.multiple_of(blocks[lax.axis_index("col"), chunk * per_chunk + i] * block, block)
        copies.append(
            pltpu.make_async_copy(
                a_hbm.at[:, pl.ds(start, block)], target.at[:, pl.ds(i * block, block)], sems.at[i]
            )
        )
    return copies


def first_kernel(blocks_hbm, counts_hbm, a_hbm, f_hbm, keep_ref, send_ref, a_1, a_2, a_3, f_high, f_low, *scratch):
    a_buf, f_buf, acc, blocks, counts, a_sems, f_sems, table_sems = scratch
    slots = f_sems.shape[0]
    tile_rows = f_buf.shape[0]
    block = tile_rows // slots
    r, c = lax.axis_index("row"), lax.axis_index("col")
    tables = [
        pltpu.make_async_copy(blocks_hbm, blocks, table_sems.at[0]),
        pltpu.make_async_copy(counts_hbm, counts, table_sems.at[1]),
    ]
    for copy in tables:
        copy.start()

    def f_copy(s):
        span = pl.ds(pl.multiple_of(s * block, block), block)
        return pltpu.make_async_copy(f_hbm.at[span, :], f_buf.at[span, :], f_sems.at[s])

    for s in range(slots):
        f_copy(s).start()
    for copy in tables:
        copy.wait()
    now, *later = [
        column_copies(ahead, blocks, a_hbm, target, a_sems.at[i])
        for i, (ahead, target) in enumerate(zip(ORDER, (a_buf, a_1, a_2, a_3)))
    ]
    for copies in (now, *later):
        for copy in copies:
            copy.start()
    own_count = counts[r]

    @pl.loop(0, slots)
    def _(s):
        f_copy(s).wait()
        rows = f_buf[pl.ds(pl.multiple_of(s * block, block), block), :]
        rows = jnp.where(s < own_count, -rows, 0.0)
        high = rows.astype(jnp.bfloat16)
        target = pl.ds(pl.multiple_of(blocks[r, s] * block, block), block)
        f_high[target, :] = high
        f_low[target, :] = (rows - high.astype(jnp.float32)).astype(jnp.bfloat16)

    for copy in now:
        copy.wait()
    chunk = chunk_of(r // 4 + ORDER[0], c)
    emit_chunk((block, counts[c]), chunk, a_buf[...], f_high, f_low, acc, keep_ref, send_ref)
    for copies in later:
        for copy in copies:
            copy.wait()


def next_kernel(step, slots, counts, a_now, f_high, f_low, keep_ref, send_ref, acc):
    block = a_now.shape[0] // slots
    c = lax.axis_index("col")
    chunk = chunk_of(lax.axis_index("row") // 4 + ORDER[step], c)
    emit_chunk((block, counts[c]), chunk, a_now[...], f_high, f_low, acc, keep_ref, send_ref)


SMEM = pl.BlockSpec(memory_space=pltpu.SMEM)
VMEM = pl.BlockSpec(memory_space=pltpu.VMEM)
HBM = pl.BlockSpec(memory_space=pltpu.HBM)
PARAMS = pltpu.CompilerParams(vmem_limit_bytes=24 * 1024 * 1024)


def chunk_products(blocks, counts, a, f, share):
    tile_rows, width = f.shape
    slots = blocks.shape[1]
    chunk_rows = tile_rows // RING
    per_chunk = slots // RING
    half = jax.ShapeDtypeStruct((2, share, width), jnp.float32)
    split = jax.ShapeDtypeStruct((tile_rows, width), jnp.bfloat16)
    columns = jax.ShapeDtypeStruct((tile_rows, chunk_rows), jnp.float32)
    acc = pltpu.VMEM((chunk_rows, width), jnp.float32)
    in_hbm = [pltpu.with_memory_space_constraint(value, pltpu.HBM) for value in (blocks, counts, a, f)]
    keep, send, *columns_of, high, low = pl.pallas_call(
        first_kernel,
        out_shape=(half, half, columns, columns, columns, split, split),
        in_specs=[HBM] * 4,
        out_specs=(VMEM,) * 7,
        scratch_shapes=[
            pltpu.VMEM((tile_rows, chunk_rows), jnp.float32),
            pltpu.VMEM((tile_rows, width), jnp.float32),
            acc,
            pltpu.SMEM(blocks.shape, jnp.int32),
            pltpu.SMEM(counts.shape, jnp.int32),
            pltpu.SemaphoreType.DMA((RING, per_chunk)),
            pltpu.SemaphoreType.DMA((slots,)),
            pltpu.SemaphoreType.DMA((2,)),
        ],
        compiler_params=PARAMS,
        name="product_0",
    )(*in_hbm)
    yield keep, send
    for step in range(1, RING):
        yield pl.pallas_call(
            functools.partial(next_kernel, step, slots),
            out_shape=(half, half),
            in_specs=[SMEM, VMEM, VMEM, VMEM],
            out_specs=(VMEM, VMEM),
            scratch_shapes=[acc],
            compiler_params=PARAMS,
        )(counts, columns_of[step - 1], high, low)


def per_device(ancestor_inverse, factor_panel, ancestor_blocks, ancestor_count):
    rows, cols = lax.axis_size("row"), lax.axis_size("col")
    width = factor_panel.shape[1]
    share_rows = factor_panel.shape[0] // rows
    along_x = rows // RING

    def to(value, target):
        return lax.ppermute(value, "row", [(i, target(i)) for i in range(rows)])

    def ahead(value):
        return to(value, lambda i: (i + along_x) % rows)

    def behind(value):
        return to(value, lambda i: (i - along_x) % rows)

    products = list(chunk_products(ancestor_blocks, ancestor_count, ancestor_inverse, factor_panel, share_rows))

    def plane_sum(keep, send):
        chip = keep + to(send, lambda i: i ^ 1)
        return chip[0] + to(chip[1], lambda i: i ^ 2)

    far, front, back, own = [plane_sum(*product) for product in products]
    half = width // 2
    from_back, from_front = ahead(far[:, :half]), behind(far[:, half:])
    plus = jnp.concatenate([front[:, :half] + from_back, front[:, half:]], axis=1)
    minus = jnp.concatenate([back[:, :half], back[:, half:] + from_front], axis=1)
    share = own + ahead(plus) + behind(minus)
    swap = [(i * cols + j, j * cols + share_of(i, j)) for i in range(rows) for j in range(cols)]
    inverse_panel = lax.ppermute(share, ("row", "col"), swap)
    features = share.T.reshape(rows, width // rows, share_rows)
    pieces = lax.all_to_all(features, "row", 0, 0, tiled=True)
    return in_order(inverse_panel, pieces)


def in_order_kernel(panel, pieces, panel_out, out):
    panel_out[...] = panel[...]
    rows = pieces.shape[0]
    c = lax.axis_index("col")
    parts = []
    for s in range(rows):
        x = (2 * (c // RING) + 2 * RING + 2 - s // RING) % RING
        parts.append(pieces[RING * x + 2 * (s % 2) + (s // 2) % 2])
    out[...] = jnp.concatenate(parts, axis=1)


def in_order(panel, pieces):
    count, height, columns = pieces.shape
    return pl.pallas_call(
        in_order_kernel,
        out_shape=(
            jax.ShapeDtypeStruct(panel.shape, panel.dtype),
            jax.ShapeDtypeStruct((height, count * columns), pieces.dtype),
        ),
        in_specs=[VMEM, VMEM],
        out_specs=(VMEM, VMEM),
        compiler_params=pltpu.CompilerParams(vmem_limit_bytes=8 * 1024 * 1024),
        name="in_order",
    )(panel, pieces)


def solution(mesh):
    return jax.shard_map(
        per_device,
        mesh=mesh,
        in_specs=(P("row", "col"), P("row", None), P(), P()),
        out_specs=(P(("row", "col"), None), P("row", "col")),
        check_vma=False,
    )
```

```python
import functools

import jax
import jax.numpy as jnp
from jax import lax
from jax.experimental import pallas as pl
from jax.experimental.pallas import tpu as pltpu
from jax.sharding import PartitionSpec as P


RING = 4
ORDER = (2, 1, 3, 0)


def chunk_of(x, c):
    return (2 * (c // RING) + 2 * RING + 2 - x) % RING


def share_of(r, c):
    return RING * chunk_of(r // RING, c) + 2 * ((r + r // 2) % 2) + (r // 2) % 2


def emit_chunk(blocks_count, chunk, a, f_high, f_low, acc, keep_ref, send_ref):
    block, count = blocks_count
    share = keep_ref.shape[1]
    rows = acc.shape[0]
    dims = (((0,), (0,)), ((), ()))

    def product(left, right):
        return lax.dot_general(left, right, dims, preferred_element_type=jnp.float32)

    high = a.astype(jnp.bfloat16)
    low = (a - high.astype(jnp.float32)).astype(jnp.bfloat16)
    total = product(low, f_high[...]) + product(high, f_low[...]) + product(high, f_high[...])
    slot = chunk * (rows // block) + lax.broadcasted_iota(jnp.int32, (rows, 1), 0) // block
    acc[...] = jnp.where(slot < count, total, 0.0)
    r = lax.axis_index("row")
    core, y = r % 2, (r // 2) % 2
    for other in range(2):
        along_y = y if other == 0 else 1 - y
        keep_ref[other] = acc[pl.ds((2 * ((core + along_y) % 2) + along_y) * share, share), :]
        send_ref[other] = acc[pl.ds((2 * ((core + along_y + 1) % 2) + along_y) * share, share), :]


def column_copies(ahead, blocks, a_hbm, target, sems):
    tile_rows, chunk_rows = target.shape
    slots = blocks.shape[1]
    block = tile_rows // slots
    per_chunk = chunk_rows // block
    chunk = chunk_of(lax.axis_index("row") // 4 + ahead, lax.axis_index("col"))
    copies = []
    for i in range(per_chunk):
        start = pl.multiple_of(blocks[lax.axis_index("col"), chunk * per_chunk + i] * block, block)
        copies.append(
            pltpu.make_async_copy(
                a_hbm.at[:, pl.ds(start, block)], target.at[:, pl.ds(i * block, block)], sems.at[i]
            )
        )
    return copies


def first_kernel(blocks_hbm, counts_hbm, a_hbm, f_hbm, keep_ref, send_ref, a_1, a_2, a_3, f_high, f_low, *scratch):
    a_buf, f_buf, acc, blocks, counts, a_sems, f_sems, table_sems = scratch
    slots = f_sems.shape[0]
    tile_rows = f_buf.shape[0]
    block = tile_rows // slots
    r, c = lax.axis_index("row"), lax.axis_index("col")
    tables = [
        pltpu.make_async_copy(blocks_hbm, blocks, table_sems.at[0]),
        pltpu.make_async_copy(counts_hbm, counts, table_sems.at[1]),
    ]
    for copy in tables:
        copy.start()

    def f_copy(s):
        span = pl.ds(pl.multiple_of(s * block, block), block)
        return pltpu.make_async_copy(f_hbm.at[span, :], f_buf.at[span, :], f_sems.at[s])

    for s in range(slots):
        f_copy(s).start()
    for copy in tables:
        copy.wait()
    now, *later = [
        column_copies(ahead, blocks, a_hbm, target, a_sems.at[i])
        for i, (ahead, target) in enumerate(zip(ORDER, (a_buf, a_1, a_2, a_3)))
    ]
    for copies in (now, *later):
        for copy in copies:
            copy.start()
    own_count = counts[r]

    @pl.loop(0, slots)
    def _(s):
        f_copy(s).wait()
        rows = f_buf[pl.ds(pl.multiple_of(s * block, block), block), :]
        rows = jnp.where(s < own_count, -rows, 0.0)
        high = rows.astype(jnp.bfloat16)
        target = pl.ds(pl.multiple_of(blocks[r, s] * block, block), block)
        f_high[target, :] = high
        f_low[target, :] = (rows - high.astype(jnp.float32)).astype(jnp.bfloat16)

    for copy in now:
        copy.wait()
    chunk = chunk_of(r // 4 + ORDER[0], c)
    emit_chunk((block, counts[c]), chunk, a_buf[...], f_high, f_low, acc, keep_ref, send_ref)
    for copies in later:
        for copy in copies:
            copy.wait()


def next_kernel(step, slots, counts, a_now, f_high, f_low, keep_ref, send_ref, acc):
    block = a_now.shape[0] // slots
    c = lax.axis_index("col")
    chunk = chunk_of(lax.axis_index("row") // 4 + ORDER[step], c)
    emit_chunk((block, counts[c]), chunk, a_now[...], f_high, f_low, acc, keep_ref, send_ref)


SMEM = pl.BlockSpec(memory_space=pltpu.SMEM)
VMEM = pl.BlockSpec(memory_space=pltpu.VMEM)
HBM = pl.BlockSpec(memory_space=pltpu.HBM)
PARAMS = pltpu.CompilerParams(vmem_limit_bytes=24 * 1024 * 1024)


def chunk_products(blocks, counts, a, f, share):
    tile_rows, width = f.shape
    slots = blocks.shape[1]
    chunk_rows = tile_rows // RING
    per_chunk = slots // RING
    half = jax.ShapeDtypeStruct((2, share, width), jnp.float32)
    split = jax.ShapeDtypeStruct((tile_rows, width), jnp.bfloat16)
    columns = jax.ShapeDtypeStruct((tile_rows, chunk_rows), jnp.float32)
    acc = pltpu.VMEM((chunk_rows, width), jnp.float32)
    in_hbm = [pltpu.with_memory_space_constraint(value, pltpu.HBM) for value in (blocks, counts, a, f)]
    keep, send, *columns_of, high, low = pl.pallas_call(
        first_kernel,
        out_shape=(half, half, columns, columns, columns, split, split),
        in_specs=[HBM] * 4,
        out_specs=(VMEM,) * 7,
        scratch_shapes=[
            pltpu.VMEM((tile_rows, chunk_rows), jnp.float32),
            pltpu.VMEM((tile_rows, width), jnp.float32),
            acc,
            pltpu.SMEM(blocks.shape, jnp.int32),
            pltpu.SMEM(counts.shape, jnp.int32),
            pltpu.SemaphoreType.DMA((RING, per_chunk)),
            pltpu.SemaphoreType.DMA((slots,)),
            pltpu.SemaphoreType.DMA((2,)),
        ],
        compiler_params=PARAMS,
        name="product_0",
    )(*in_hbm)
    yield keep, send
    for step in range(1, RING):
        yield pl.pallas_call(
            functools.partial(next_kernel, step, slots),
            out_shape=(half, half),
            in_specs=[SMEM, VMEM, VMEM, VMEM],
            out_specs=(VMEM, VMEM),
            scratch_shapes=[acc],
            compiler_params=PARAMS,
        )(counts, columns_of[step - 1], high, low)


def per_device(ancestor_inverse, factor_panel, ancestor_blocks, ancestor_count):
    rows, cols = lax.axis_size("row"), lax.axis_size("col")
    width = factor_panel.shape[1]
    share_rows = factor_panel.shape[0] // rows
    along_x = rows // RING

    def to(value, target):
        return lax.ppermute(value, "row", [(i, target(i)) for i in range(rows)])

    def ahead(value):
        return to(value, lambda i: (i + along_x) % rows)

    def behind(value):
        return to(value, lambda i: (i - along_x) % rows)

    products = list(chunk_products(ancestor_blocks, ancestor_count, ancestor_inverse, factor_panel, share_rows))

    def plane_sum(keep, send):
        chip = keep + to(send, lambda i: i ^ 1)
        return chip[0] + to(chip[1], lambda i: i ^ 2)

    far, front, back, own = [plane_sum(*product) for product in products]
    half = width // 2
    from_back, from_front = ahead(far[:, :half]), behind(far[:, half:])
    plus = jnp.concatenate([front[:, :half] + from_back, front[:, half:]], axis=1)
    minus = jnp.concatenate([back[:, :half], back[:, half:] + from_front], axis=1)
    share = own + ahead(plus) + behind(minus)
    swap = [(i * cols + j, j * cols + share_of(i, j)) for i in range(rows) for j in range(cols)]
    inverse_panel = lax.ppermute(share, ("row", "col"), swap)
    features = share.T.reshape(rows, width // rows, share_rows)
    pieces = lax.all_to_all(features, "row", 0, 0, tiled=True)
    return in_order(inverse_panel, pieces)


def in_order_kernel(panel, pieces, panel_out, out):
    panel_out[...] = panel[...]
    rows = pieces.shape[0]
    c = lax.axis_index("col")
    parts = []
    for s in range(rows):
        x = (2 * (c // RING) + 2 * RING + 2 - s // RING) % RING
        parts.append(pieces[RING * x + 2 * (s % 2) + (s + s // 2) % 2])
    out[...] = jnp.concatenate(parts, axis=1)


def in_order(panel, pieces):
    count, height, columns = pieces.shape
    return pl.pallas_call(
        in_order_kernel,
        out_shape=(
            jax.ShapeDtypeStruct(panel.shape, panel.dtype),
            jax.ShapeDtypeStruct((height, count * columns), pieces.dtype),
        ),
        in_specs=[VMEM, VMEM],
        out_specs=(VMEM, VMEM),
        compiler_params=pltpu.CompilerParams(vmem_limit_bytes=8 * 1024 * 1024),
        name="in_order",
    )(panel, pieces)


def solution(mesh):
    return jax.shard_map(
        per_device,
        mesh=mesh,
        in_specs=(P("row", "col"), P("row", None), P(), P()),
        out_specs=(P(("row", "col"), None), P("row", "col")),
        check_vma=False,
    )
```
